32 devices in a mesh: dom: 8 (over z, x), blk: 4 (over y, core).
Axes of the slice: x: 2, y: 2, z: 4, core: 2. Of those that a mesh axis runs over, the one named last changes fastest.
Arguments:
- multipliers: float32 [4, 48, 64, 256], P('blk', 'dom'), may hold values from -6 to 6
- residual: float32 [4, 48, 64, 256], P('blk', 'dom')
- dir_prev: float32 [4, 48, 64, 256], P('blk', 'dom'), may hold values from -6 to 6
- rho_prev: float32 [64], replicated, may hold values from 10 to 100
- face_ids: int32 [4, 16, 6], P('blk'), may hold values from 0 to 47, as said below
- face_sign: int32 [4, 16, 6], P('blk'), may hold values from -1 to 1, as said below
- dual_blocks: bfloat16 [4, 16, 1536, 1536], P('blk', 'dom'), as said below
- dirichlet_blocks: bfloat16 [4, 16, 1536, 1536], P('blk', 'dom'), as said below
- coupling: bfloat16 [4, 16, 256, 1536], P('blk', 'dom'), may hold values from -0.15625 to 0.15625
- corner_ids: int32 [4, 16, 256], P('blk', 'dom'), may hold values from 0 to 3071, as said below
- coarse_inv: bfloat16 [8, 4, 768, 768], P('dom', 'blk'), as said below
Outputs:
- new_multipliers: float32 [4, 48, 64, 256], P('blk', 'dom')
- new_residual: float32 [4, 48, 64, 256], P('blk', 'dom')
- direction: float32 [4, 48, 64, 256], P('blk', 'dom')
- rho_now: float32 [64], replicated
- reduction: float32 [64], replicated
The draws below stay inside these ranges and needn't reach their ends.
Inputs may be any that keep to these rules, and one draw needn't show every extreme that they name: `face_ids`: in each column b every face index below 48 is named by exactly two slots, of subdomains held by two different indices of dom; face f is owned by dom index f // 6. The 2 subdomains of one dom index name at most 3 faces of any one owner, and in every column some pairs of a dom index and an owner reach 3. `face_sign`: of the two slots that name one face, one has +1 and the other -1. `dual_blocks`: each block is symmetric positive definite. `dirichlet_blocks`: each block is symmetric positive definite. `coarse_inv`: each block is symmetric positive definite. `corner_ids`: the corners of one subdomain are distinct, and corner k lies in coarse block k // 64, that is, its index n satisfies n // 768 = k // 64.
All inputs are finite; a program needn't handle non-finite values.
Results may differ from the reference program's by a relative error of at most 0.033.
Values may be sent and summed in bfloat16 or wider, within the bound.
A program may use at most 128 MiB of HBM per device.

```python
import math
import jax
import jax.numpy as jnp
from jax import lax

FDOF = 256
CASES = 64
FPS = 6
SUB_DEV = 2
CB = 768
NCD = 256
LOCAL = 1536
FACE_DEV = 6
CAP = 3
NSC = 16
NFC = 48
N_DOM = 8
N_BLK = 4


def face_pattern(key):
    base_key = jax.random.fold_in(key, 5)
    slot_total = FPS * SUB_DEV

    def shuffled(place_key_one):
        return jax.random.permutation(place_key_one, slot_total)

    def column_pattern(column_key):
        perm_key, place_key = jax.random.split(column_key)
        offsets_perm = jax.random.permutation(perm_key, N_DOM)
        element = jnp.arange(slot_total)
        cycle_index = 1 + jnp.maximum(element - CAP, 0) % (N_DOM - 1)
        offsets = jnp.where(element < CAP, offsets_perm[0], offsets_perm[cycle_index])
        dom_rows = jnp.arange(N_DOM)
        owner = (dom_rows[:, None] - offsets[None, :]) % N_DOM
        faces = owner * FACE_DEV + (element % FACE_DEV)[None, :]
        signs = jnp.broadcast_to(jnp.where(element < FACE_DEV, 1, -1)[None, :], (N_DOM, slot_total))
        place_keys = jax.random.split(place_key, N_DOM)
        placement = jax.vmap(shuffled)(place_keys)
        inverse = jnp.argsort(placement, axis=1, stable=True)
        faces = jnp.take_along_axis(faces, inverse, axis=1)
        signs = jnp.take_along_axis(signs, inverse, axis=1)
        return (faces.reshape(N_DOM * SUB_DEV, FPS).astype(jnp.int32), signs.reshape(N_DOM * SUB_DEV, FPS).astype(jnp.int32))
    column_keys = jax.random.split(base_key, N_BLK)
    return jax.vmap(column_pattern)(column_keys)


def draw_face_ids(key, part):
    return face_pattern(key)[0]


def draw_face_sign(key, part):
    return face_pattern(key)[1]


def draw_corner_ids(key, part):
    base_key = jax.random.fold_in(key, 31)
    share = NCD // N_BLK
    count = N_BLK * N_DOM * SUB_DEV * N_BLK
    keys = jax.random.split(base_key, count)

    def one_perm(perm_key):
        return jax.random.permutation(perm_key, CB)[:share]
    picks = jax.vmap(one_perm)(keys).reshape(N_BLK, N_DOM * SUB_DEV, N_BLK, share)
    sub_index = jnp.arange(N_DOM * SUB_DEV)[None, :, None, None]
    block_index = jnp.arange(N_BLK)[None, None, :, None]
    first = picks[:, :, :, :1]
    shift_high = jnp.where((sub_index == 0) & (block_index == N_BLK - 1), CB - 1 - first, 0)
    shift_low = jnp.where((sub_index == 0) & (block_index == 0), -first, 0)
    moved = (picks + shift_high + shift_low) % CB
    ids = moved + block_index * CB
    return ids.reshape(N_BLK, N_DOM * SUB_DEV, NCD).astype(jnp.int32)


def spd_stack(key, leading, matrix_order):
    block_count = leading[0] * leading[1]

    def single_block(block_index):
        block_key = jax.random.fold_in(key, block_index)
        noise_key, diag_key = jax.random.split(block_key)
        noise_vals = jax.random.normal(noise_key, (matrix_order, matrix_order), jnp.float32)
        symmetric = (noise_vals + noise_vals.T) * (0.7 / math.sqrt(2.0 * matrix_order))
        diagonal = jnp.exp(jax.random.uniform(diag_key, (matrix_order,), jnp.float32, math.log(2.2), math.log(4.4)))
        return (symmetric + jnp.diag(diagonal)).astype(jnp.bfloat16)
    blocks = lax.map(single_block, jnp.arange(block_count))
    return blocks.reshape(leading + (matrix_order, matrix_order))


def draw_dual_blocks(key, part):
    return spd_stack(jax.random.fold_in(key, 21), (N_BLK, N_DOM * SUB_DEV), FPS * FDOF)


def draw_dirichlet_blocks(key, part):
    return spd_stack(jax.random.fold_in(key, 22), (N_BLK, N_DOM * SUB_DEV), FPS * FDOF)


def draw_coarse_inv(key, part):
    return spd_stack(jax.random.fold_in(key, 23), (N_DOM, N_BLK), CB)


def draw_residual(key, part):
    noise_key = jax.random.fold_in(key, 11)
    shape = (N_BLK, N_DOM * FACE_DEV, CASES, FDOF)
    owner = (jnp.arange(N_DOM * FACE_DEV) // FACE_DEV).astype(jnp.float32)
    column = jnp.arange(N_BLK).astype(jnp.float32)
    rise = (1.0 + 2.0 * owner / (N_DOM - 1))[None, :, None, None] * (1.0 + 0.5 * column / max(N_BLK - 1, 1))[:, None, None, None]
    base_vals = jax.random.normal(noise_key, shape, jnp.float32)
    return (base_vals * rise).astype(jnp.float32)


def steps_of(rng, extent, shards, least, high):
    gain, own = 1.0, jax.random.fold_in(rng, 6)
    for position, parts in shards:
        steps = jnp.exp(jax.random.uniform(jax.random.fold_in(own, position), (parts,), jnp.float32, least / len(shards), high / len(shards)))
        gain = gain * jnp.repeat(steps, extent[position] // parts).reshape([-1 if axis == position else 1 for axis in range(len(extent))])
    return gain


def noise(stream_key, extent, scale, most, cuts=(), held_as=jnp.bfloat16):
    result = jax.random.normal(stream_key, extent, jnp.float32) * scale
    if len(cuts) > 0:
        result = steps_of(stream_key, extent, cuts, -0.22, 0.18) * result
    return jnp.clip(result, min=-most, max=most).astype(held_as)


def setup_inputs(seed: int = 0) -> dict:
    key_list = jax.random.split(jax.random.key(seed), 12)
    return {
        "multipliers": noise(key_list[0], (N_BLK, NFC, CASES, FDOF), 1.0, 6.0, ((0, 4), (1, 8)), jnp.float32),
        "residual": draw_residual(jax.random.fold_in(key_list[11], 71), 0),
        "dir_prev": noise(key_list[2], (N_BLK, NFC, CASES, FDOF), 1.0, 6.0, ((0, 4), (1, 8)), jnp.float32),
        "rho_prev": jnp.clip(jnp.exp(jax.random.uniform(key_list[3], (CASES,), jnp.float32, math.log(10.0), math.log(100.0))), 10.0, 100.0),
        "face_ids": draw_face_ids(jax.random.fold_in(key_list[11], 71), 0),
        "face_sign": draw_face_sign(jax.random.fold_in(key_list[11], 71), 0),
        "dual_blocks": draw_dual_blocks(jax.random.fold_in(key_list[11], 71), 0),
        "dirichlet_blocks": draw_dirichlet_blocks(jax.random.fold_in(key_list[11], 71), 0),
        "coupling": noise(key_list[8], (N_BLK, NSC, NCD, LOCAL), LOCAL ** -0.5, 0.15625, ((0, 4), (1, 8))),
        "corner_ids": draw_corner_ids(jax.random.fold_in(key_list[11], 71), 0),
        "coarse_inv": draw_coarse_inv(jax.random.fold_in(key_list[11], 71), 0),
    }


def pull_slots(vector, face_ids, face_sign):
    vector_half = vector.astype(jnp.bfloat16)

    def column_pick(column_vec, column_ids):
        return column_vec[column_ids]

    picked = jax.vmap(column_pick)(vector_half, face_ids)
    return picked * face_sign.astype(jnp.bfloat16)[:, :, :, None, None]


def local_products(slots, matrices):
    def column_product(operands):
        pieces, blocks = operands
        wide = blocks.astype(jnp.float32).reshape(N_DOM * SUB_DEV, FPS, FDOF, FPS * FDOF)
        return jnp.einsum("stcx,stxm->scm", pieces.astype(jnp.float32), wide)

    return lax.map(column_product, (slots, matrices))


def push_faces(totals, face_ids, face_sign):
    per_slot = totals.reshape(N_BLK, N_DOM * SUB_DEV, CASES, FPS, FDOF)
    per_slot = per_slot * face_sign.astype(jnp.float32)[:, :, None, :, None]
    rounded = lax.optimization_barrier(per_slot.astype(jnp.bfloat16)).astype(jnp.float32)
    rounded = jnp.transpose(rounded, (0, 1, 3, 2, 4)).reshape(N_BLK, N_DOM * SUB_DEV * FPS, CASES, FDOF)

    def column_add(column_ids, column_vals):
        start_sums = jnp.zeros((N_DOM * FACE_DEV, CASES, FDOF), jnp.float32)
        return start_sums.at[column_ids.reshape(-1)].add(column_vals)

    return jax.vmap(column_add)(face_ids, rounded)


def coarse_term(slots, coupling, corner_ids, coarse_inv):
    wide = coupling.astype(jnp.float32).reshape(N_BLK, N_DOM * SUB_DEV, NCD, FPS, FDOF)
    corner_terms = jnp.einsum("bjtcx,bjktx->bjck", slots.astype(jnp.float32), wide)
    corner_terms = corner_terms.reshape(N_BLK, N_DOM, SUB_DEV, CASES, NCD)
    index_rows = corner_ids.reshape(N_BLK, N_DOM, SUB_DEV, NCD)

    def column_assemble(column_terms, column_index):
        values = jnp.transpose(column_terms, (2, 0, 1, 3)).reshape(CASES, N_BLK * SUB_DEV * NCD)
        start_sums = jnp.zeros((CASES, N_BLK * CB), jnp.float32)
        return start_sums.at[:, column_index.reshape(-1)].add(values)

    coarse_rhs = jax.vmap(column_assemble, in_axes=(1, 1))(corner_terms, index_rows)
    coarse_half = lax.optimization_barrier(coarse_rhs.astype(jnp.bfloat16))
    coarse_half = coarse_half.astype(jnp.float32).reshape(N_DOM, CASES, N_BLK, CB)
    solved = jnp.einsum("dcbm,dbmn->dcbn", coarse_half, coarse_inv.astype(jnp.float32))
    solved = lax.optimization_barrier(solved.astype(jnp.bfloat16))
    solved = solved.astype(jnp.float32).reshape(N_DOM, CASES, N_BLK * CB)

    def column_pick(column_sol, column_index):
        return column_sol[:, column_index]

    picked = jax.vmap(column_pick, in_axes=(0, 1))(solved, index_rows)
    picked = jnp.transpose(picked, (2, 0, 3, 1, 4)).reshape(N_BLK, N_DOM * SUB_DEV, CASES, NCD)
    return jnp.einsum("bjck,bjkl->bjcl", picked, coupling.astype(jnp.float32))


def reference(multipliers, residual, dir_prev, rho_prev, face_ids, face_sign, dual_blocks, dirichlet_blocks, coupling, corner_ids, coarse_inv):
    total_count = N_BLK * N_DOM * FACE_DEV * FDOF
    slots = pull_slots(residual, face_ids, face_sign)
    precond_res = push_faces(local_products(slots, dirichlet_blocks), face_ids, face_sign)
    rho_now = jnp.sum(residual * precond_res, axis=(0, 1, 3)) / total_count
    res_mean = jnp.sum(residual * residual, axis=(0, 1, 3)) / total_count
    beta_ratio = rho_now / rho_prev
    direction = precond_res + beta_ratio[None, None, :, None] * dir_prev
    slots = pull_slots(direction, face_ids, face_sign)
    totals = local_products(slots, dual_blocks) + coarse_term(slots, coupling, corner_ids, coarse_inv)
    image = push_faces(totals, face_ids, face_sign)
    curvature = jnp.sum(direction * image, axis=(0, 1, 3)) / total_count
    alpha_step = rho_now / curvature
    new_multipliers = multipliers + alpha_step[None, None, :, None] * direction
    new_residual = residual - alpha_step[None, None, :, None] * image
    reduction = (jnp.sum(new_residual * new_residual, axis=(0, 1, 3)) / total_count) / res_mean
    return new_multipliers, new_residual, direction, rho_now, reduction
```

```python
import functools

import jax
import jax.numpy as jnp
from jax import lax
from jax.experimental import pallas as pl
from jax.experimental.pallas import tpu as pltpu
from jax.sharding import PartitionSpec as P

MESH = pl.DeviceIdType.MESH
IN_VMEM = pl.BlockSpec(memory_space=pltpu.VMEM)


def peers_of(axis):
    count, me = lax.axis_size(axis), lax.axis_index(axis)
    return [(k - 1, lax.rem(me + k, count)) for k in range(1, count)]


def meet(axes):
    barrier = pltpu.get_barrier_semaphore()
    total = 0
    for axis in axes:
        for _, peer in peers_of(axis):
            pl.semaphore_signal(barrier, inc=1, device_id={axis: peer}, device_id_type=MESH)
            total += 1
    pl.semaphore_wait(barrier, total)


def remote(src, dst, send, recv, axis, peer):
    return pltpu.make_async_remote_copy(
        src_ref=src, dst_ref=dst, send_sem=send, recv_sem=recv,
        device_id={axis: peer}, device_id_type=MESH,
    )


def sum_kernel(x_ref, o_ref, dom_slots, part, blk_slots, send_d, recv_d, send_b, recv_b):
    meet(("dom", "blk"))
    source = x_ref
    for axis, slots, send, recv in (
        ("dom", dom_slots, send_d, recv_d),
        ("blk", blk_slots, send_b, recv_b),
    ):
        me = lax.axis_index(axis)
        copies = [
            remote(source, slots.at[me], send.at[k], recv.at[k], axis, peer)
            for k, peer in peers_of(axis)
        ]
        for copy in copies:
            copy.start()
        slots[me] = source[...]
        for copy in copies:
            copy.wait()
        total = slots[0]
        for index in range(1, lax.axis_size(axis)):
            total = total + slots[index]
        if axis == "dom":
            part[...] = total
            source = part
        else:
            o_ref[...] = total


def sum_everywhere(rows, collective_id):
    case_count = rows[0].shape[0]
    width = -(-case_count // 128) * 128
    tile = jnp.pad(jnp.stack(rows), ((0, 8 - len(rows)), (0, width - case_count)))
    n_dom, n_blk = lax.axis_size("dom"), lax.axis_size("blk")
    dma = pltpu.SemaphoreType.DMA
    sums = pl.pallas_call(
        sum_kernel,
        out_shape=jax.ShapeDtypeStruct(tile.shape, jnp.float32),
        in_specs=[IN_VMEM],
        out_specs=IN_VMEM,
        scratch_shapes=[
            pltpu.VMEM((n_dom,) + tile.shape, jnp.float32),
            pltpu.VMEM(tile.shape, jnp.float32),
            pltpu.VMEM((n_blk,) + tile.shape, jnp.float32),
            dma((n_dom - 1,)), dma((n_dom - 1,)), dma((n_blk - 1,)), dma((n_blk - 1,)),
        ],
        compiler_params=pltpu.CompilerParams(collective_id=collective_id, has_side_effects=True),
    )(tile)
    return [sums[i, :case_count] for i in range(len(rows))]


def exchange_kernel(x_ref, o_ref, send, recv, own):
    meet(("dom",))
    me = lax.axis_index("dom")
    copies = [
        remote(x_ref.at[peer], o_ref.at[me], send.at[k], recv.at[k], "dom", peer)
        for k, peer in peers_of("dom")
    ]
    for copy in copies:
        copy.start()
    mine = pltpu.make_async_copy(x_ref.at[me], o_ref.at[me], own)
    mine.start()
    for copy in copies:
        copy.wait()
    mine.wait()


def exchange(x, collective_id):
    n_dom = lax.axis_size("dom")
    dma = pltpu.SemaphoreType.DMA
    return pl.pallas_call(
        exchange_kernel,
        out_shape=jax.ShapeDtypeStruct(x.shape, x.dtype),
        in_specs=[IN_VMEM],
        out_specs=IN_VMEM,
        scratch_shapes=[dma((n_dom - 1,)), dma((n_dom - 1,)), dma],
        compiler_params=pltpu.CompilerParams(collective_id=collective_id, has_side_effects=True),
    )(x)


def coarse_kernel(
    terms_ref, ids_ref, inv_ref, o_ref, terms, ids, parts, picks,
    send_t, recv_t, send_i, recv_i, send_p, recv_p,
):
    meet(("blk",))
    n_blk, me = lax.axis_size("blk"), lax.axis_index("blk")
    span = inv_ref.shape[0]
    copies = []
    for k, peer in peers_of("blk"):
        copies.append(remote(ids_ref.at[peer], ids.at[me], send_i.at[k], recv_i.at[k], "blk", peer))
        copies.append(remote(terms_ref.at[peer], terms.at[me], send_t.at[k], recv_t.at[k], "blk", peer))
    for copy in copies:
        copy.start()
    terms[me] = terms_ref[me]
    ids[me] = ids_ref[me]
    for copy in copies:
        copy.wait()

    def hot(index):
        rows = lax.broadcasted_iota(jnp.int32, (span, ids.shape[2]), 0)
        return (rows == ids[index][:1, :]).astype(jnp.float32).astype(jnp.bfloat16)

    rhs = jnp.zeros((terms.shape[1], span), jnp.float32)
    for index in range(n_blk):
        rhs += lax.dot_general(
            terms[index], hot(index), (((1,), (1,)), ((), ())), preferred_element_type=jnp.float32
        )
    solved = jnp.dot(
        rhs.astype(jnp.bfloat16), inv_ref[...], preferred_element_type=jnp.float32
    ).astype(jnp.bfloat16)
    for index in range(n_blk):
        parts[index] = jnp.dot(
            solved, hot(index), preferred_element_type=jnp.float32
        ).astype(jnp.bfloat16)
    copies = [
        remote(parts.at[peer], picks.at[me], send_p.at[k], recv_p.at[k], "blk", peer)
        for k, peer in peers_of("blk")
    ]
    for copy in copies:
        copy.start()
    picks[me] = parts[me]
    for copy in copies:
        copy.wait()
    o_ref[...] = picks[...]


def coarse_picks(terms, ids, inverse, collective_id):
    n_blk = lax.axis_size("blk")
    dma = pltpu.SemaphoreType.DMA
    return pl.pallas_call(
        coarse_kernel,
        out_shape=jax.ShapeDtypeStruct(terms.shape, jnp.bfloat16),
        in_specs=[IN_VMEM] * 3,
        out_specs=IN_VMEM,
        scratch_shapes=[
            pltpu.VMEM(terms.shape, jnp.bfloat16),
            pltpu.VMEM(ids.shape, jnp.int32),
            pltpu.VMEM(terms.shape, jnp.bfloat16),
            pltpu.VMEM(terms.shape, jnp.bfloat16),
        ] + [dma((n_blk - 1,))] * 6,
        compiler_params=pltpu.CompilerParams(collective_id=collective_id, has_side_effects=True),
    )(terms, ids, inverse)


def block_product(pieces, matrices):
    sub_count, face_slots, case_count, face_len = pieces.shape
    blocks = matrices.reshape(sub_count, face_slots, face_len, matrices.shape[-1])
    return jnp.einsum("stcx,stxm->scm", pieces, blocks, preferred_element_type=jnp.float32)


def corner_products(pieces, coupling_rows):
    sub_count, face_slots, case_count, face_len = pieces.shape
    blocks = coupling_rows.reshape(sub_count, coupling_rows.shape[1], face_slots, face_len)
    return jnp.einsum("stcx,sktx->sck", pieces, blocks, preferred_element_type=jnp.float32)


def on_device(
    multipliers,
    residual,
    dir_prev,
    rho_prev,
    face_ids,
    face_sign,
    dual_blocks,
    dirichlet_blocks,
    coupling,
    corner_ids,
    coarse_inv,
):
    n_dom = lax.axis_size("dom")
    n_blk = lax.axis_size("blk")
    my_index = lax.axis_index("dom")
    faces_dev = multipliers.shape[1]
    case_count = multipliers.shape[2]
    face_len = multipliers.shape[3]
    sub_count = dual_blocks.shape[1]
    face_slots = face_ids.shape[2]
    slot_count = sub_count * face_slots
    column_ids = face_ids[0].reshape(n_dom, slot_count)
    column_sign = face_sign[0].reshape(n_dom, slot_count)
    my_sign = lax.dynamic_index_in_dim(column_sign, my_index, 0, keepdims=False).astype(
        jnp.bfloat16
    )
    capacity = (slot_count + n_dom - 1) // n_dom + 1
    owners = column_ids // faces_dev
    slot_order = jnp.arange(slot_count)
    earlier = (owners[:, :, None] == owners[:, None, :]) & (
        slot_order[None, None, :] < slot_order[None, :, None]
    )
    slot_rank = jnp.sum(earlier.astype(jnp.int32), axis=2)
    places = jnp.arange(capacity)
    peer_index = jnp.arange(n_dom)
    face_index = jnp.arange(faces_dev)
    owned_here = (owners == my_index)[:, :, None, None]
    rank_match = slot_rank[:, :, None, None] == places[None, None, :, None]
    face_match = (column_ids % faces_dev)[:, :, None, None] == face_index[None, None, None, :]
    send_table = jnp.sum((owned_here & rank_match & face_match).astype(jnp.int32), axis=1).astype(
        jnp.bfloat16
    )
    my_owner = lax.dynamic_index_in_dim(owners, my_index, 0, keepdims=False)
    my_rank = lax.dynamic_index_in_dim(slot_rank, my_index, 0, keepdims=False)
    pull_match = (my_owner[:, None, None] == peer_index[None, :, None]) & (
        my_rank[:, None, None] == places[None, None, :]
    )
    pull_table = (pull_match.astype(jnp.bfloat16) * my_sign[:, None, None]).reshape(
        sub_count, face_slots, n_dom, capacity
    )

    def fetch_multiply(vector_half, matrices, with_coarse, collective_id):

        def finish(pieces):
            product = block_product(pieces, matrices)
            if with_coarse:
                return (product, corner_products(pieces, coupling[0]))
            return product

        outgoing = jnp.einsum(
            "dkf,fcx->dkcx", send_table, vector_half, preferred_element_type=jnp.float32
        ).astype(jnp.bfloat16)
        pieces = jnp.einsum(
            "stok,okcx->stcx",
            pull_table,
            exchange(outgoing, collective_id),
            preferred_element_type=jnp.float32,
        ).astype(jnp.bfloat16)
        return finish(pieces)

    def return_sums(totals, collective_id):
        per_slot = totals.reshape(sub_count, case_count, face_slots, face_len).astype(jnp.bfloat16)
        outgoing = jnp.einsum(
            "stok,sctx->okcx", pull_table, per_slot, preferred_element_type=jnp.float32
        ).astype(jnp.bfloat16)
        incoming = exchange(outgoing, collective_id)
        summed = jnp.einsum(
            "dkf,dkcx->fcx", send_table, incoming, preferred_element_type=jnp.float32
        )
        return summed

    total_count = n_dom * n_blk * faces_dev * face_len
    residual_rows = residual[0]
    precond_res = return_sums(
        fetch_multiply(residual_rows.astype(jnp.bfloat16), dirichlet_blocks[0], False, 0), 1
    )
    rho_sum, square_sum = sum_everywhere(
        (
            jnp.sum(residual_rows * precond_res, axis=(0, 2)),
            jnp.sum(residual_rows * residual_rows, axis=(0, 2)),
        ),
        2,
    )
    rho_now = rho_sum / total_count
    res_mean = square_sum / total_count
    beta_ratio = rho_now / rho_prev
    direction = precond_res + beta_ratio[None, :, None] * dir_prev[0]
    product, corner_terms = fetch_multiply(direction.astype(jnp.bfloat16), dual_blocks[0], True, 3)
    corner_count = corner_terms.shape[2]
    share = corner_count // n_blk
    block_span = coarse_inv.shape[2]
    by_block = jnp.transpose(
        corner_terms.astype(jnp.bfloat16).reshape(sub_count, case_count, n_blk, share), (2, 1, 0, 3)
    ).reshape(n_blk, case_count, sub_count * share)
    block_ids = jnp.transpose(
        (corner_ids[0] % block_span).reshape(sub_count, n_blk, share), (1, 0, 2)
    ).reshape(n_blk, 1, sub_count * share)
    block_ids = jnp.broadcast_to(block_ids, (n_blk, 8, sub_count * share))
    picks = coarse_picks(by_block, block_ids, coarse_inv[0, 0], 4)
    picked = jnp.transpose(
        picks.reshape(n_blk, case_count, sub_count, share), (2, 1, 0, 3)
    ).reshape(sub_count, case_count, corner_count)
    image_vec = return_sums(
        product
        + jnp.einsum("sck,skl->scl", picked, coupling[0], preferred_element_type=jnp.float32),
        5,
    )
    curve_sum, cross_sum, image_sum = sum_everywhere(
        (
            jnp.sum(direction * image_vec, axis=(0, 2)),
            jnp.sum(residual_rows * image_vec, axis=(0, 2)),
            jnp.sum(image_vec * image_vec, axis=(0, 2)),
        ),
        6,
    )
    alpha_step = rho_now / (curve_sum / total_count)
    new_res = residual_rows - alpha_step[None, :, None] * image_vec
    new_sum = square_sum - 2.0 * alpha_step * cross_sum + alpha_step * alpha_step * image_sum
    reduction = new_sum / total_count / res_mean
    new_lam = multipliers[0] + alpha_step[None, :, None] * direction
    return (new_lam[None], new_res[None], direction[None], rho_now, reduction)


def solution(mesh):
    in_specs = (
        P("blk", "dom", None, None),
        P("blk", "dom", None, None),
        P("blk", "dom", None, None),
        P(),
        P("blk", None, None),
        P("blk", None, None),
        P("blk", "dom", None, None),
        P("blk", "dom", None, None),
        P("blk", "dom", None, None),
        P("blk", "dom", None),
        P("dom", "blk", None, None),
    )
    out_specs = (
        P("blk", "dom", None, None),
        P("blk", "dom", None, None),
        P("blk", "dom", None, None),
        P(),
        P(),
    )
    return jax.shard_map(
        on_device, mesh=mesh, in_specs=in_specs, out_specs=out_specs, check_vma=False
    )
```

```python
import jax
import jax.numpy as jnp
from jax import lax
from jax.experimental import pallas as pl
from jax.experimental.pallas import tpu as pltpu
from jax.sharding import PartitionSpec as P

MESH = pl.DeviceIdType.MESH
F32, BF16 = jnp.float32, jnp.bfloat16


def peers_of(axis):
    count, me = lax.axis_size(axis), lax.axis_index(axis)
    return [(k - 1, lax.rem(me + k, count)) for k in range(1, count)]


def remote(src, dst, send, recv, axis, peer):
    return pltpu.make_async_remote_copy(
        src_ref=src, dst_ref=dst, send_sem=send, recv_sem=recv,
        device_id={axis: peer}, device_id_type=MESH,
    )


def step_kernel(
    send_face, pull_slot, push_slot, first, second, sign,
    lam_ref, res_ref, dir_ref, rho_ref, ids_ref,
    dirichlet, dual, coupling, inverse,
    new_lam, new_res, new_dir, stats,
    w_dir, w_dual, w_cpl, w_inv, outs, in_0, in_1, in_2, in_3, slots, per_slot, image,
    dom_sums, part, blk_sums, ids, terms_out, terms_in, picks_out, picks_in,
    load, send_x, recv_x, send_s, recv_s, send_t, recv_t, send_c, recv_c,
):
    n_dom, n_blk = lax.axis_size("dom"), lax.axis_size("blk")
    me, my_blk = lax.axis_index("dom"), lax.axis_index("blk")
    faces, cases, face_len = res_ref.shape
    subs = slots.shape[0]
    fps = slots.shape[2] // face_len
    cap = send_face.shape[0] // n_dom
    count = n_dom * n_blk * faces * face_len
    share = ids.shape[3]
    ins = (in_0, in_1, in_2, in_3)
    span = w_inv.shape[0]

    loads = [
        pltpu.make_async_copy(src, dst, load.at[i])
        for i, (src, dst) in enumerate(
            ((dirichlet, w_dir), (coupling, w_cpl), (dual, w_dual), (inverse, w_inv))
        )
    ]
    for copy in loads:
        copy.start()

    barrier = pltpu.get_barrier_semaphore()
    for axis in ("dom", "blk"):
        for _, peer in peers_of(axis):
            pl.semaphore_signal(barrier, inc=1, device_id={axis: peer}, device_id_type=MESH)
    pl.semaphore_wait(barrier, n_dom + n_blk - 2)

    def exchange(turn, value_at):
        copies = []
        for k, peer in peers_of("dom"):
            for place in range(cap):
                outs[turn, peer * cap + place] = value_at(peer * cap + place)
            copy = remote(
                outs.at[turn, pl.ds(peer * cap, cap)], ins[turn].at[pl.ds(me * cap, cap)],
                send_x.at[turn, k], recv_x.at[turn, k], "dom", peer,
            )
            copy.start()
            copies.append(copy)
        for place in range(cap):
            ins[turn][me * cap + place] = value_at(me * cap + place)
        return copies

    def finish(copies):
        for copy in copies:
            copy.wait()

    def pull(turn, vector):
        return exchange(turn, lambda i: vector[send_face[i]].astype(BF16))

    def to_slots(turn):
        for s in range(subs):
            for t in range(fps):
                i = s * fps + t
                value = ins[turn][pull_slot[i]].astype(F32) * sign[i]
                slots[s, :, t * face_len:(t + 1) * face_len] = value.astype(BF16)

    def product(weights, s, t):
        return jnp.dot(
            slots[s], weights[s, :, t * face_len:(t + 1) * face_len], preferred_element_type=F32
        )

    def push(turn):
        return exchange(turn, lambda i: per_slot[push_slot[i]])

    def face_sum(turn, f):
        return ins[turn][first[f]].astype(F32) + ins[turn][second[f]].astype(F32)

    def as_rows(columns):
        lanes = part.shape[2]
        place = lax.broadcasted_iota(jnp.int32, (cases, 128), 1)
        tile = jnp.zeros((cases, 128), F32)
        for i, column in enumerate(columns):
            tile = jnp.where(place == i, column, tile)
        if lanes > cases:
            tile = jnp.concatenate([tile, jnp.zeros((lanes - cases, 128), F32)], axis=0)
        return jnp.transpose(tile)[:8]

    def as_column(row):
        tile = jnp.concatenate([row, jnp.zeros((127, row.shape[1]), F32)], axis=0)
        return jnp.transpose(tile)[:cases, :1]

    def total_of(turn, columns):
        part[2 * turn] = as_rows(columns)
        for level, axis, sums, base in (
            (0, "dom", dom_sums, 0), (1, "blk", blk_sums, n_dom - 1),
        ):
            here = lax.axis_index(axis)
            source = 2 * turn + level
            copies = [
                remote(
                    part.at[source], sums.at[turn, here],
                    send_s.at[turn, base + k], recv_s.at[turn, base + k], axis, peer,
                )
                for k, peer in peers_of(axis)
            ]
            for copy in copies:
                copy.start()
            sums[turn, here] = part[source]
            finish(copies)
            total = sums[turn, 0]
            for index in range(1, lax.axis_size(axis)):
                total = total + sums[turn, index]
            if level == 0:
                part[source + 1] = total
        return total

    def lane_sum(value):
        return jnp.sum(value, axis=1, keepdims=True)

    pulled = pull(0, res_ref)
    id_copies = [
        remote(ids_ref.at[peer], ids.at[my_blk], send_c.at[0, k], recv_c.at[0, k], "blk", peer)
        for k, peer in peers_of("blk")
    ]
    for copy in id_copies:
        copy.start()
    ids[my_blk] = ids_ref[my_blk]
    square = jnp.zeros((cases, face_len), F32)
    for f in range(faces):
        square += res_ref[f] * res_ref[f]
    loads[0].wait()
    finish(pulled)
    to_slots(0)
    for s in range(subs):
        for t in range(fps):
            i = s * fps + t
            per_slot[i] = (product(w_dir, s, t) * sign[i]).astype(BF16)
    finish(push(1))
    rho_part = jnp.zeros((cases, face_len), F32)
    for f in range(faces):
        value = face_sum(1, f)
        image[f] = value
        rho_part += res_ref[f] * value
    first_total = total_of(0, (lane_sum(rho_part), lane_sum(square)))
    rho_now = first_total[0:1] / count
    square_sum = first_total[1:2]
    beta = as_column(rho_now / rho_ref[0:1])
    for f in range(faces):
        new_dir[f] = image[f] + beta * dir_ref[f]

    pulled = pull(2, new_dir)
    loads[1].wait()
    loads[2].wait()
    loads[3].wait()
    finish(id_copies)
    finish(pulled)
    to_slots(2)
    for b in range(n_blk):
        for s in range(subs):
            terms_out[b, s] = lax.dot_general(
                slots[s], w_cpl[s, b * share:(b + 1) * share, :], (((1,), (1,)), ((), ())),
                preferred_element_type=F32,
            ).astype(BF16)
    copies = [
        remote(terms_out.at[peer], terms_in.at[my_blk], send_t.at[0, k], recv_t.at[0, k], "blk", peer)
        for k, peer in peers_of("blk")
    ]
    for copy in copies:
        copy.start()
    terms_in[my_blk] = terms_out[my_blk]
    sums = [[product(w_dual, s, t) for t in range(fps)] for s in range(subs)]
    finish(copies)

    def hot(p, s):
        rows = lax.broadcasted_iota(jnp.int32, (span, share), 0)
        return (rows == ids[p, s][:1, :]).astype(F32).astype(BF16)

    rhs = jnp.zeros((cases, span), F32)
    for p in range(n_blk):
        for s in range(subs):
            rhs += lax.dot_general(
                terms_in[p, s], hot(p, s), (((1,), (1,)), ((), ())), preferred_element_type=F32
            )
    solved = jnp.dot(rhs.astype(BF16), w_inv[...], preferred_element_type=F32).astype(BF16)
    for p in range(n_blk):
        for s in range(subs):
            picks_out[p, s] = jnp.dot(solved, hot(p, s), preferred_element_type=F32).astype(BF16)
    copies = [
        remote(picks_out.at[peer], picks_in.at[my_blk], send_t.at[1, k], recv_t.at[1, k], "blk", peer)
        for k, peer in peers_of("blk")
    ]
    for copy in copies:
        copy.start()
    picks_in[my_blk] = picks_out[my_blk]
    finish(copies)
    for s in range(subs):
        for t in range(fps):
            i = s * fps + t
            value = sums[s][t]
            for b in range(n_blk):
                value += jnp.dot(
                    picks_in[b, s],
                    w_cpl[s, b * share:(b + 1) * share, t * face_len:(t + 1) * face_len],
                    preferred_element_type=F32,
                )
            per_slot[i] = (value * sign[i]).astype(BF16)
    finish(push(3))
    curve = jnp.zeros((cases, face_len), F32)
    cross = jnp.zeros((cases, face_len), F32)
    norm = jnp.zeros((cases, face_len), F32)
    for f in range(faces):
        value = face_sum(3, f)
        image[f] = value
        curve += new_dir[f] * value
        cross += res_ref[f] * value
        norm += value * value
    last_total = total_of(1, (lane_sum(curve), lane_sum(cross), lane_sum(norm)))
    alpha = rho_now / (last_total[0:1] / count)
    new_sum = square_sum - 2.0 * alpha * last_total[1:2] + alpha * alpha * last_total[2:3]
    stats[0:1] = rho_now
    stats[1:2] = (new_sum / count) / (square_sum / count)
    stats[2:8] = jnp.zeros((6, stats.shape[1]), F32)
    step = as_column(alpha)
    for f in range(faces):
        new_lam[f] = lam_ref[f] + step * new_dir[f]
        new_res[f] = res_ref[f] - step * image[f]


def on_device(
    multipliers, residual, dir_prev, rho_prev, face_ids, face_sign,
    dual_blocks, dirichlet_blocks, coupling, corner_ids, coarse_inv,
):
    n_dom, n_blk = lax.axis_size("dom"), lax.axis_size("blk")
    me = lax.axis_index("dom")
    _, faces, cases, face_len = multipliers.shape
    _, subs, local, _ = dual_blocks.shape
    slot_count = subs * face_ids.shape[2]
    column_ids = face_ids[0].reshape(n_dom, slot_count)
    signs = face_sign[0].reshape(n_dom, slot_count)
    cap = (slot_count + n_dom - 1) // n_dom + 1
    owners = column_ids // faces
    order = jnp.arange(slot_count)
    earlier = (owners[:, :, None] == owners[:, None, :]) & (order[None, None, :] < order[None, :, None])
    rank = jnp.sum(earlier.astype(jnp.int32), axis=2)
    places = jnp.arange(cap)
    mine = ((owners == me)[:, :, None]) & (rank[:, :, None] == places)
    send_face = jnp.sum(jnp.where(mine, (column_ids % faces)[:, :, None], 0), axis=1).reshape(-1)
    code = jnp.arange(n_dom)[:, None] * cap + rank
    match = (column_ids - me * faces)[:, :, None] == jnp.arange(faces)
    first = jnp.min(jnp.where(match, code[:, :, None], n_dom * cap - 1), axis=(0, 1))
    second = jnp.max(jnp.where(match, code[:, :, None], 0), axis=(0, 1))
    my_owner = lax.dynamic_index_in_dim(owners, me, 0, keepdims=False)
    my_rank = lax.dynamic_index_in_dim(rank, me, 0, keepdims=False)
    my_sign = lax.dynamic_index_in_dim(signs, me, 0, keepdims=False).astype(F32)
    pull_slot = my_owner * cap + my_rank
    push_slot = jnp.sum(
        jnp.where(pull_slot[None, :] == jnp.arange(n_dom * cap)[:, None], order[None, :], 0), axis=1
    )
    span = coarse_inv.shape[2]
    corners = coupling.shape[2]
    share = corners // n_blk
    block_ids = jnp.transpose((corner_ids[0] % span).reshape(subs, n_blk, share), (1, 0, 2))
    block_ids = jnp.broadcast_to(block_ids[:, :, None, :], (n_blk, subs, 8, share))
    lanes = -(-cases // 128) * 128
    rho_tile = jnp.broadcast_to(
        jnp.pad(rho_prev, (0, lanes - cases), constant_values=1.0)[None, :], (8, lanes)
    )
    field = jax.ShapeDtypeStruct((faces, cases, face_len), F32)
    vmem = pl.BlockSpec(memory_space=pltpu.VMEM)
    smem = pl.BlockSpec(memory_space=pltpu.SMEM)
    hbm = pl.BlockSpec(memory_space=pl.ANY)
    dma = pltpu.SemaphoreType.DMA
    dom_peers, blk_peers = n_dom - 1, n_blk - 1
    terms = pltpu.VMEM((n_blk, subs, cases, share), BF16)
    piece = (n_dom * cap, cases, face_len)
    new_lam, new_res, new_dir, stats = pl.pallas_call(
        step_kernel,
        out_shape=(field, field, field, jax.ShapeDtypeStruct((8, lanes), F32)),
        in_specs=[smem] * 6 + [vmem] * 5 + [hbm] * 4,
        out_specs=(vmem,) * 4,
        scratch_shapes=[
            pltpu.VMEM((subs, local, local), BF16),
            pltpu.VMEM((subs, local, local), BF16),
            pltpu.VMEM((subs, corners, local), BF16),
            pltpu.VMEM((span, span), BF16),
            pltpu.VMEM((4,) + piece, BF16),
            *[pltpu.VMEM(piece, BF16)] * 4,
            pltpu.VMEM((subs, cases, local), BF16),
            pltpu.VMEM((slot_count, cases, face_len), BF16),
            pltpu.VMEM((faces, cases, face_len), F32),
            pltpu.VMEM((2, n_dom, 8, lanes), F32),
            pltpu.VMEM((4, 8, lanes), F32),
            pltpu.VMEM((2, n_blk, 8, lanes), F32),
            pltpu.VMEM((n_blk, subs, 8, share), jnp.int32),
            terms, terms, terms, terms,
            dma((4,)),
            dma((4, dom_peers)), dma((4, dom_peers)),
            dma((2, dom_peers + blk_peers)), dma((2, dom_peers + blk_peers)),
            dma((2, blk_peers)), dma((2, blk_peers)),
            dma((1, blk_peers)), dma((1, blk_peers)),
        ],
        compiler_params=pltpu.CompilerParams(
            collective_id=0, has_side_effects=True, vmem_limit_bytes=60 << 20
        ),
    )(
        send_face, pull_slot, push_slot, first, second, my_sign,
        multipliers[0], residual[0], dir_prev[0], rho_tile, block_ids,
        dirichlet_blocks[0], dual_blocks[0], coupling[0], coarse_inv[0, 0],
    )
    return new_lam[None], new_res[None], new_dir[None], stats[0, :cases], stats[1, :cases]


def solution(mesh):
    in_specs = (
        P("blk", "dom", None, None),
        P("blk", "dom", None, None),
        P("blk", "dom", None, None),
        P(),
        P("blk", None, None),
        P("blk", None, None),
        P("blk", "dom", None, None),
        P("blk", "dom", None, None),
        P("blk", "dom", None, None),
        P("blk", "dom", None),
        P("dom", "blk", None, None),
    )
    out_specs = (
        P("blk", "dom", None, None),
        P("blk", "dom", None, None),
        P("blk", "dom", None, None),
        P(),
        P(),
    )
    return jax.shard_map(
        on_device, mesh=mesh, in_specs=in_specs, out_specs=out_specs, check_vma=False
    )
```
